32 devices in a mesh: tm: 8 (over z, y), pair: 4 (over x, core).
Axes of the slice: x: 2, y: 2, z: 4, core: 2. Of those that a mesh axis runs over, the one named last changes fastest.
Arguments:
- x_path: bfloat16 [8, 4096, 512], P('pair', 'tm'), parts along dimension 0, may hold values from -0.19921875 to 0.19921875
- x_anchor: bfloat16 [8, 512], P('pair'), parts along dimension 0, may hold values from -0.19921875 to 0.19921875
- y_steps: bfloat16 [8, 1024, 512], P('pair', 'tm'), parts along dimension 0, may hold values from -0.14941406 to 0.14941406
- left_in: float32 [16, 4096], P('pair', 'tm'), parts along dimension 0, may hold values from 0.5 to 1.5
- bottom_in: float32 [16, 1024], P('pair', 'tm'), parts along dimension 0, may hold values from 0.5 to 1.5
- corner_in: float32 [16, 8], P('pair', 'tm'), parts along dimension 0, may hold values from 0.5 to 1.5
Outputs:
- right_out: float32 [16, 4096], P('pair', 'tm'), parts along dimension 0
- top_out: float32 [16, 6144], P('pair', 'tm'), parts along dimension 0
The draws below stay inside these ranges and needn't reach their ends.
There are 4 independent parts, one for each index of `pair`. The reference program is written for one: setup_inputs(seed, part) draws one part's arguments, and reference() takes and returns one part's arrays. A program takes and returns all parts, laid end to end along the dimension named above; each array names one. Nothing has to cross between parts.
All inputs are finite; a program needn't handle non-finite values.
Results may differ from the reference program's by a relative error of at most 0.00094.
Values may be sent and summed in bfloat16 or wider, within the bound.
No kernel may reach another device: no remote copies, remote signals or barrier semaphores. Data moves between devices by JAX's collectives and lax.ppermute only.
A program may use at most 64 MiB of HBM per device.

```python
import jax
import jax.numpy as jnp
from jax import lax

CH = 512
TILE = 128
TX = 512
SX = 2
SY = 2
TICKS = 6
PASSES = 4
PAIRS = 4
XLEN = 4096
YLEN = 1024
N_TM = 8


def steps_of(key, dims, shards, low, largest):
    loudness = 1.0
    for position, parts in shards:
        draws = jax.random.uniform(jax.random.fold_in(jax.random.fold_in(key, 6), position), (parts,), jnp.float32, low / len(shards), largest / len(shards))
        loudness = loudness * jnp.repeat(jnp.exp(draws), dims[position] // parts).reshape((-1,) + (1,) * (len(dims) - 1 - position))
    return loudness


def bell_draw(stream_key, extent, deviation, bound, split=(), kind=jnp.bfloat16):
    loudness = steps_of(stream_key, extent, split, -0.22, 0.18) if split else 1.0
    array = jax.random.normal(stream_key, extent, jnp.float32) * deviation * loudness
    return jnp.minimum(jnp.maximum(array, -bound), bound).astype(kind)


def setup_inputs(seed: int = 0, part: int = 0) -> dict:
    seeds = jax.random.split(jax.random.key(seed), 7)
    part_keys = jax.random.split(jax.random.fold_in(seeds[6], part), 7)
    x_path = bell_draw(part_keys[0], (SX, XLEN, CH), 0.03, 0.19921875, ((1, 8),))
    x_anchor = bell_draw(part_keys[1], (SX, CH), 0.03, 0.19921875)
    y_steps = bell_draw(part_keys[2], (SY, YLEN, CH), 0.02, 0.14941406, ((1, 8),))
    left_in = jnp.clip(0.5 + 1.0 * jax.random.uniform(part_keys[3], (PAIRS, XLEN), jnp.float32) ** steps_of(part_keys[3], (PAIRS, XLEN), ((1, 8),), -0.2, 0.2), 0.5, 1.5)
    bottom_in = jnp.clip(0.5 + 1.0 * jax.random.uniform(part_keys[4], (PAIRS, YLEN), jnp.float32) ** steps_of(part_keys[4], (PAIRS, YLEN), ((1, 8),), -0.2, 0.2), 0.5, 1.5)
    corner_in = jnp.clip(0.5 + 1.0 * jax.random.uniform(part_keys[5], (PAIRS, N_TM), jnp.float32) ** steps_of(part_keys[5], (PAIRS, N_TM), ((1, 8),), -0.2, 0.2), 0.5, 1.5)
    return {"x_path": x_path, "x_anchor": x_anchor, "y_steps": y_steps, "left_in": left_in, "bottom_in": bottom_in, "corner_in": corner_in}


def picard(left_edge, bottom, corner, products, lower_ones):
    initial = left_edge[..., :, None] + bottom[..., None, :] - corner[..., None, None]
    kernel_grid = initial
    lower_row = jnp.concatenate([corner[..., None], bottom[..., :-1]], axis=-1)[..., None, :]
    for sweep in range(PASSES):
        inner_rows = jnp.concatenate([left_edge[..., :-1, None], kernel_grid[..., :-1, :-1]], axis=-1)
        node_values = jnp.concatenate([lower_row, inner_rows], axis=-2)
        partial_value = jnp.einsum("ab,...bc->...ac", lower_ones, node_values * products, precision=lax.Precision.HIGHEST)
        kernel_grid = initial + jnp.einsum("...ac,dc->...ad", partial_value, lower_ones, precision=lax.Precision.HIGHEST)
    return kernel_grid


def reference(x_path, x_anchor, y_steps, left_in, bottom_in, corner_in):
    count_tm = N_TM
    earlier = jnp.concatenate([x_anchor[:, None, :], x_path[:, :-1, :]], axis=1)
    steps_x = (x_path.astype(jnp.float32) - earlier.astype(jnp.float32)).astype(jnp.bfloat16)
    x_blocks = steps_x.reshape(SX, count_tm, TX, CH).astype(jnp.float32)
    y_blocks = y_steps.reshape(SY, count_tm, TILE, CH)
    positions = jnp.arange(TILE)
    lower_ones = (positions[:, None] >= positions[None, :]).astype(jnp.float32)
    row_count = TX // TILE
    left_edges = left_in.reshape(PAIRS, count_tm, TX).transpose(1, 0, 2)
    bottom = bottom_in.reshape(PAIRS, count_tm, TILE).transpose(1, 0, 2)
    corner = corner_in.transpose(1, 0)
    bottom_row = jnp.arange(count_tm)[:, None] == 0
    bottom = jnp.where(bottom_row[:, :, None], jnp.float32(1.0), bottom)
    corner = jnp.where(bottom_row, jnp.float32(1.0), corner)
    top_edges = []
    top_edge = bottom
    for tick_index in range(TICKS):
        if tick_index > 0:
            corner = bottom[..., -1]
            bottom = jnp.concatenate([jnp.ones((1, PAIRS, TILE), jnp.float32), top_edge[:-1]], axis=0)
        y_now = jnp.roll(y_blocks, tick_index, axis=1).astype(jnp.float32)
        products = jnp.einsum("xisc,yitc->ixyst", x_blocks, y_now, precision=lax.Precision.HIGHEST)
        products = products.reshape(count_tm, PAIRS, TX, TILE)
        bottom_now = bottom
        corner_now = corner
        rights = []
        for level in range(row_count):
            left_edge = left_edges[..., level * TILE:(level + 1) * TILE]
            kernel_grid = picard(left_edge, bottom_now, corner_now, products[:, :, level * TILE:(level + 1) * TILE, :], lower_ones)
            rights.append(kernel_grid[..., :, -1])
            corner_now = left_edge[..., -1]
            bottom_now = kernel_grid[..., -1, :]
        top_edge = bottom_now
        top_edges.append(top_edge)
        left_edges = jnp.concatenate(rights, axis=-1)
    right_out = left_edges.transpose(1, 0, 2).reshape(PAIRS, count_tm * TX)
    top_out = jnp.stack(top_edges, axis=2).transpose(1, 0, 2, 3).reshape(PAIRS, count_tm * TICKS * TILE)
    return right_out, top_out
```

```python
import functools

import jax
import jax.numpy as jnp
from jax import lax
from jax.experimental import pallas as pl
from jax.experimental.pallas import tpu as pltpu
from jax.sharding import PartitionSpec as P

TICKS = 6
PASSES = 4
SUB = 8


def shifted(x, axis, by):
    count = lax.axis_size(axis)
    pairs = [(i, i + by) for i in range(count) if 0 <= i + by < count]
    return lax.ppermute(x, axis, pairs)


def passed_along(x, axis, by):
    count = lax.axis_size(axis)
    return lax.ppermute(x, axis, [(i, (i + by) % count) for i in range(count)])


def two_halves(x):
    high = x.astype(jnp.bfloat16)
    low = (x - high.astype(jnp.float32)).astype(jnp.bfloat16)
    return jnp.concatenate([high, low], axis=1)


def tick_kernel(
    last, start_ref, dx_ref, y_ref, bottom_ref, before_ref, left_ref, out_ref, top_ref, products_ref
):
    series_x, block_len, channels = dx_ref.shape
    series_y, tile, _ = y_ref.shape
    pairs = series_x * series_y
    levels = block_len // tile
    groups = tile // SUB

    y_all = y_ref[...].reshape(series_y * tile, channels)
    for m in range(series_x):
        both = lax.dot_general(
            dx_ref[m], y_all, (((1,), (1,)), ((), ())), preferred_element_type=jnp.float32
        )
        for n in range(series_y):
            products_ref[m * series_y + n] = both[:, n * tile : (n + 1) * tile]

    row = lax.broadcasted_iota(jnp.int32, (2 * tile, tile), 0) % tile
    col = lax.broadcasted_iota(jnp.int32, (2 * tile, tile), 1)
    strict = (row < col).astype(jnp.float32).astype(jnp.bfloat16)
    inclusive = (row <= col).astype(jnp.float32).astype(jnp.bfloat16)
    ones = jnp.ones((2 * tile, tile), jnp.bfloat16)
    edge_sums = jnp.concatenate([strict, inclusive], axis=1)
    sub = lax.broadcasted_iota(jnp.int32, (SUB, tile), 0)
    lane = lax.broadcasted_iota(jnp.int32, (SUB, tile), 1)
    at_start = start_ref[0] == 1

    def sum_before(total):
        out = jnp.where(sub >= 1, pltpu.roll(total, 1, 0), 0.0)
        step = 1
        while step < SUB - 1:
            out = out + jnp.where(sub >= step, pltpu.roll(out, step, 0), 0.0)
            step *= 2
        return out

    def over_sublanes(x):
        step = SUB // 2
        while step:
            x = x + pltpu.roll(x, step, 0)
            step //= 2
        return x

    def dot(a, b):
        return jnp.dot(a, b, preferred_element_type=jnp.float32)

    bottom, bottom_shift, corner = [], [], []
    for p in range(pairs):
        b = jnp.broadcast_to(bottom_ref[p : p + 1, :], (SUB, tile))
        b = jnp.where(at_start, 1.0, b)
        c = jnp.broadcast_to(before_ref[p : p + 1, tile - 1 : tile], (SUB, tile))
        c = jnp.where(at_start, 1.0, c)
        bottom.append(b)
        corner.append(c)
        bottom_shift.append(jnp.where(lane == 0, c, pltpu.roll(b, 1, 1)))

    for r in range(levels):
        edge, end = [], []
        for p in range(pairs):
            left = [left_ref[p, r, j] for j in range(groups)]
            first = jnp.where(sub == 0, corner[p], pltpu.roll(left[-1], 1, 0))
            edge.append([x - corner[p] for x in [first] + left[:-1]])
            end.append(jnp.broadcast_to(left[-1][SUB - 1 : SUB, :], (SUB, tile)))
        node = [[e + bottom_shift[p] for e in edge[p]] for p in range(pairs)]
        for sweep in range(PASSES):
            weighted = [
                [
                    node[p][j] * products_ref[p, pl.ds(r * tile + j, SUB, stride=groups), :]
                    for j in range(groups)
                ]
                for p in range(pairs)
            ]
            if sweep == PASSES - 1:
                break
            for p in range(pairs):
                along = dot(two_halves(jnp.concatenate(weighted[p], axis=0)), strict)
                along = [along[j * SUB : (j + 1) * SUB] for j in range(groups)]
                running = [None, along[0]]
                for j in range(1, groups):
                    running.append(running[-1] + along[j])
                offset = sum_before(running[-1]) + bottom_shift[p]
                node[p] = [edge[p][0] + offset] + [
                    (running[j] + edge[p][j]) + offset for j in range(1, groups)
                ]
        for p in range(pairs):
            column = weighted[p]
            while len(column) > 1:
                column = [a + b for a, b in zip(column[::2], column[1::2])]
            column = over_sublanes(column[0])
            sums = dot(two_halves(column), edge_sums)
            lift = end[p] - corner[p]
            rows = dot(two_halves(jnp.concatenate(weighted[p], axis=0)), ones)
            rows = [rows[j * SUB : (j + 1) * SUB] for j in range(groups)]
            running = [rows[0]]
            for j in range(1, groups):
                running.append(running[-1] + rows[j])
            far = jnp.broadcast_to(bottom[p][:, tile - 1 : tile], (SUB, tile)) - corner[p]
            offset = sum_before(running[-1]) + far
            right = [left_ref[p, r, j] + (running[j] + offset) for j in range(groups)]
            if last:
                found = None
                for j in range(groups):
                    here = jnp.where(lane == sub * groups + j, right[j], 0.0)
                    found = here if found is None else found + here
                found = over_sublanes(found)
                out_ref[p : p + 1, r * tile : (r + 1) * tile] = found[0:1]
            else:
                for j in range(groups):
                    out_ref[p, r, j] = right[j]
            bottom[p] = bottom[p] + lift + sums[:, tile:]
            bottom_shift[p] = bottom_shift[p] + lift + sums[:, :tile]
            corner[p] = end[p]
    for p in range(pairs):
        top_ref[p : p + 1, :] = bottom[p][0:1]


def tick(start, dx, y, bottom, before, left, last):
    pairs, tile = bottom.shape
    block_len = dx.shape[1]
    vmem = pl.BlockSpec(memory_space=pltpu.VMEM)
    if last:
        left_out = jax.ShapeDtypeStruct((pairs, block_len), jnp.float32)
    else:
        left_out = jax.ShapeDtypeStruct(left.shape, jnp.float32)
    return pl.pallas_call(
        functools.partial(tick_kernel, last),
        out_shape=(left_out, jax.ShapeDtypeStruct((pairs, tile), jnp.float32)),
        in_specs=[pl.BlockSpec(memory_space=pltpu.SMEM)] + [vmem] * 5,
        out_specs=(vmem, vmem),
        scratch_shapes=[pltpu.VMEM((pairs, block_len, tile), jnp.float32)],
        name="tick_last" if last else "tick",
    )(start, dx, y, bottom, before, left)


def local(x_path, x_anchor, y_steps, left_in, bottom_in, corner_in):
    series_x, block_len, channels = x_path.shape
    series_y, tile, _ = y_steps.shape
    pairs = series_x * series_y
    levels = block_len // tile
    groups = tile // SUB
    at_start = lax.axis_index("tm") == 0
    start = at_start.astype(jnp.int32).reshape(1)
    received = shifted(x_path[:, -1:, :], "tm", 1)
    before = jnp.where(at_start, x_anchor[:, None, :], received)
    earlier = jnp.concatenate([before, x_path[:, :-1, :]], axis=1)
    dx = (x_path.astype(jnp.float32) - earlier.astype(jnp.float32)).astype(jnp.bfloat16)
    left = left_in.reshape(pairs, levels, SUB, groups).transpose(0, 1, 3, 2)
    left = jnp.broadcast_to(left[..., None], left.shape + (tile,))
    bottom = bottom_in
    previous = jnp.broadcast_to(corner_in, (pairs, tile))
    y_now = y_steps
    tops = []
    for t in range(TICKS):
        y_next = passed_along(y_now, "tm", 1) if t < TICKS - 1 else None
        left, top = tick(start, dx, y_now, bottom, previous, left, t == TICKS - 1)
        tops.append(top)
        if t < TICKS - 1:
            previous, bottom = bottom, shifted(top, "tm", 1)
            y_now = y_next
    return left, jnp.concatenate(tops, axis=1)


def solution(mesh):
    placed = (
        P("pair", "tm", None),
        P("pair", None),
        P("pair", "tm", None),
        P("pair", "tm"),
        P("pair", "tm"),
        P("pair", "tm"),
    )
    return jax.shard_map(
        local,
        mesh=mesh,
        in_specs=placed,
        out_specs=(P("pair", "tm"), P("pair", "tm")),
        check_vma=False,
    )
```

```python
import functools

import jax
import jax.numpy as jnp
from jax import lax
from jax.experimental import pallas as pl
from jax.experimental.pallas import tpu as pltpu
from jax.sharding import PartitionSpec as P


TICKS = 6
PASSES = 4
SUB = 8
VMEM_BYTES = 16 * 1024 * 1024


def shifted(x, axis, by):
    count = lax.axis_size(axis)
    pairs = [(i, i + by) for i in range(count) if 0 <= i + by < count]
    return lax.ppermute(x, axis, pairs)


def passed_along(x, axis, by):
    count = lax.axis_size(axis)
    return lax.ppermute(x, axis, [(i, (i + by) % count) for i in range(count)])


def two_halves(x):
    high = x.astype(jnp.bfloat16)
    low = (x - high.astype(jnp.float32)).astype(jnp.bfloat16)
    return jnp.concatenate([high, low], axis=1)


def prep_kernel(x_ref, anchor_ref, left_ref, dx_ref, edge_ref, head_ref):
    series_x, _, _ = x_ref.shape
    pairs, levels, groups, _, tile = edge_ref.shape
    for m in range(series_x):
        x = x_ref[m].astype(jnp.float32)
        head_ref[m] = x[0:SUB]
        first = lax.broadcasted_iota(jnp.int32, x.shape, 0) == 0
        anchor = jnp.broadcast_to(anchor_ref[m : m + 1, :].astype(jnp.float32), x.shape)
        dx_ref[m] = (x - jnp.where(first, anchor, pltpu.roll(x, 1, 0))).astype(jnp.bfloat16)
    sub = lax.broadcasted_iota(jnp.int32, (SUB, tile), 0)
    lane = lax.broadcasted_iota(jnp.int32, (SUB, tile), 1)
    for p in range(pairs):
        for r in range(levels):
            row = jnp.broadcast_to(left_ref[p : p + 1, r * tile : (r + 1) * tile], (SUB, tile))
            for j in range(groups):
                own = jnp.where(lane == sub * groups + j, row, 0.0)
                edge_ref[p, r, j] = jnp.broadcast_to(
                    jnp.sum(own, axis=1, keepdims=True), (SUB, tile)
                )


def tick_kernel(at, last, *refs):
    start_ref, dx_ref, y_ref, bottom_ref, before_ref, left_ref, *refs = refs
    if at == 0:
        head_ref, received_ref, *refs = refs
    else:
        row_ref, *refs = refs
    earlier_refs = []
    if last:
        earlier_refs, refs = refs[:at], refs[at:]
    out_ref, top_ref, *refs = refs
    if not last:
        after_ref, *refs = refs
    if at == 0:
        row_ref, *refs = refs
    (products_ref,) = refs
    series_x, block_len, channels = dx_ref.shape
    series_y, tile, _ = y_ref.shape
    pairs = series_x * series_y
    levels = block_len // tile
    groups = tile // SUB
    at_start = start_ref[0] == 1

    if at == 0:
        for m in range(series_x):
            jump = head_ref[m] - received_ref[m].astype(jnp.float32)
            row_ref[m] = jnp.where(at_start, dx_ref[m, 0:SUB, :].astype(jnp.float32), jump)
    y_all = y_ref[...].reshape(series_y * tile, channels)
    for m in range(series_x):
        both = lax.dot_general(
            dx_ref[m], y_all, (((1,), (1,)), ((), ())), preferred_element_type=jnp.float32
        )
        for n in range(series_y):
            products_ref[m * series_y + n] = both[:, n * tile : (n + 1) * tile]
        both = lax.dot_general(
            row_ref[m].astype(jnp.bfloat16),
            y_all,
            (((1,), (1,)), ((), ())),
            preferred_element_type=jnp.float32,
        )
        for n in range(series_y):
            products_ref[m * series_y + n, 0:1, :] = both[0:1, n * tile : (n + 1) * tile]

    row = lax.broadcasted_iota(jnp.int32, (2 * tile, tile), 0) % tile
    col = lax.broadcasted_iota(jnp.int32, (2 * tile, tile), 1)
    strict = (row < col).astype(jnp.float32).astype(jnp.bfloat16)
    inclusive = (row <= col).astype(jnp.float32).astype(jnp.bfloat16)
    ones = jnp.ones((2 * tile, tile), jnp.bfloat16)
    edge_sums = jnp.concatenate([strict, inclusive], axis=1)
    sub = lax.broadcasted_iota(jnp.int32, (SUB, tile), 0)
    lane = lax.broadcasted_iota(jnp.int32, (SUB, tile), 1)

    def sum_before(total):
        out = jnp.where(sub >= 1, pltpu.roll(total, 1, 0), 0.0)
        step = 1
        while step < SUB - 1:
            out = out + jnp.where(sub >= step, pltpu.roll(out, step, 0), 0.0)
            step *= 2
        return out

    def over_sublanes(x):
        step = SUB // 2
        while step:
            x = x + pltpu.roll(x, step, 0)
            step //= 2
        return x

    def dot(a, b):
        return jnp.dot(a, b, preferred_element_type=jnp.float32)

    bottom, bottom_shift, corner = [], [], []
    for p in range(pairs):
        b = jnp.broadcast_to(bottom_ref[p : p + 1, :], (SUB, tile))
        b = jnp.where(at_start, 1.0, b)
        c = jnp.broadcast_to(before_ref[p : p + 1, tile - 1 : tile], (SUB, tile))
        c = jnp.where(at_start, 1.0, c)
        bottom.append(b)
        corner.append(c)
        if not last:
            after_ref[p : p + 1, :] = b[0:1]
        bottom_shift.append(jnp.where(lane == 0, c, pltpu.roll(b, 1, 1)))

    for r in range(levels):
        edge, end = [], []
        for p in range(pairs):
            left = [left_ref[p, r, j] for j in range(groups)]
            first = jnp.where(sub == 0, corner[p], pltpu.roll(left[-1], 1, 0))
            edge.append([x - corner[p] for x in [first] + left[:-1]])
            end.append(jnp.broadcast_to(left[-1][SUB - 1 : SUB, :], (SUB, tile)))
        node = [[e + bottom_shift[p] for e in edge[p]] for p in range(pairs)]
        for sweep in range(PASSES):
            weighted = [
                [
                    node[p][j] * products_ref[p, pl.ds(r * tile + j, SUB, stride=groups), :]
                    for j in range(groups)
                ]
                for p in range(pairs)
            ]
            if sweep == PASSES - 1:
                break
            for p in range(pairs):
                along = dot(two_halves(jnp.concatenate(weighted[p], axis=0)), strict)
                along = [along[j * SUB : (j + 1) * SUB] for j in range(groups)]
                running = [None, along[0]]
                for j in range(1, groups):
                    running.append(running[-1] + along[j])
                offset = sum_before(running[-1]) + bottom_shift[p]
                node[p] = [edge[p][0] + offset] + [
                    (running[j] + edge[p][j]) + offset for j in range(1, groups)
                ]
        for p in range(pairs):
            column = weighted[p]
            while len(column) > 1:
                column = [a + b for a, b in zip(column[::2], column[1::2])]
            column = over_sublanes(column[0])
            sums = dot(two_halves(column), edge_sums)
            lift = end[p] - corner[p]
            rows = dot(two_halves(jnp.concatenate(weighted[p], axis=0)), ones)
            rows = [rows[j * SUB : (j + 1) * SUB] for j in range(groups)]
            running = [rows[0]]
            for j in range(1, groups):
                running.append(running[-1] + rows[j])
            far = jnp.broadcast_to(bottom[p][:, tile - 1 : tile], (SUB, tile)) - corner[p]
            offset = sum_before(running[-1]) + far
            right = [left_ref[p, r, j] + (running[j] + offset) for j in range(groups)]
            if last:
                found = None
                for j in range(groups):
                    here = jnp.where(lane == sub * groups + j, right[j], 0.0)
                    found = here if found is None else found + here
                found = over_sublanes(found)
                out_ref[p : p + 1, r * tile : (r + 1) * tile] = found[0:1]
            else:
                for j in range(groups):
                    out_ref[p, r, j] = right[j]
            bottom[p] = bottom[p] + lift + sums[:, tile:]
            bottom_shift[p] = bottom_shift[p] + lift + sums[:, :tile]
            corner[p] = end[p]
    for k, earlier_ref in enumerate(earlier_refs):
        top_ref[:, k * tile : (k + 1) * tile] = earlier_ref[...]
    begin = len(earlier_refs) * tile
    for p in range(pairs):
        top_ref[p : p + 1, begin : begin + tile] = bottom[p][0:1]


VMEM = pl.BlockSpec(memory_space=pltpu.VMEM)


def prepare(x_path, x_anchor, left_in, tile):
    pairs, block_len = left_in.shape
    edge = (pairs, block_len // tile, tile // SUB, SUB, tile)
    return pl.pallas_call(
        prep_kernel,
        out_shape=(
            jax.ShapeDtypeStruct(x_path.shape, jnp.bfloat16),
            jax.ShapeDtypeStruct(edge, jnp.float32),
            jax.ShapeDtypeStruct((x_path.shape[0], SUB, x_path.shape[2]), jnp.float32),
        ),
        in_specs=[VMEM] * 3,
        out_specs=(VMEM, VMEM, VMEM),
        compiler_params=pltpu.CompilerParams(vmem_limit_bytes=VMEM_BYTES),
        name="prep",
    )(x_path, x_anchor, left_in)


def tick(at, last, start, dx, y, bottom, before, left, first, tops):
    pairs, tile = bottom.shape
    series_x, block_len, channels = dx.shape
    edge = jax.ShapeDtypeStruct((pairs, tile), jnp.float32)
    if last:
        shapes = [
            jax.ShapeDtypeStruct((pairs, block_len), jnp.float32),
            jax.ShapeDtypeStruct((pairs, tile * (at + 1)), jnp.float32),
        ]
        first = first + tops
    else:
        shapes = [jax.ShapeDtypeStruct(left.shape, jnp.float32), edge, edge]
    if at == 0:
        shapes.append(jax.ShapeDtypeStruct((series_x, SUB, channels), jnp.float32))
    specs = [pl.BlockSpec(memory_space=pltpu.SMEM)] + [VMEM] * (5 + len(first))
    return pl.pallas_call(
        functools.partial(tick_kernel, at, last),
        out_shape=tuple(shapes),
        in_specs=specs,
        out_specs=(VMEM,) * len(shapes),
        scratch_shapes=[pltpu.VMEM((pairs, block_len, tile), jnp.float32)],
        compiler_params=pltpu.CompilerParams(vmem_limit_bytes=VMEM_BYTES),
        name="tick",
    )(start, dx, y, bottom, before, left, *first)


def local(x_path, x_anchor, y_steps, left_in, bottom_in, corner_in):
    tile = y_steps.shape[1]
    at_start = lax.axis_index("tm") == 0
    start = at_start.astype(jnp.int32).reshape(1)
    received = shifted(x_path[:, -1:, :], "tm", 1)
    y_next = passed_along(y_steps, "tm", 1)
    dx, left, head = prepare(x_path, x_anchor, left_in, tile)
    y_now, bottom = y_steps, bottom_in
    previous = jnp.broadcast_to(corner_in, bottom_in.shape)
    first, tops = [head, received], []
    for t in range(TICKS):
        last = t == TICKS - 1
        left, top, *rest = tick(t, last, start, dx, y_now, bottom, previous, left, first, tops)
        if last:
            return left, top
        tops.append(top)
        previous = rest[0]
        if t == 0:
            first = [rest[1]]
        bottom = shifted(top, "tm", 1)
        y_now = y_next
        if t + 2 < TICKS:
            y_now, _ = lax.optimization_barrier((y_now, top))
            y_next = passed_along(y_now, "tm", 1)


def solution(mesh):
    placed = (
        P("pair", "tm", None),
        P("pair", None),
        P("pair", "tm", None),
        P("pair", "tm"),
        P("pair", "tm"),
        P("pair", "tm"),
    )
    return jax.shard_map(
        local,
        mesh=mesh,
        in_specs=placed,
        out_specs=(P("pair", "tm"), P("pair", "tm")),
        check_vma=False,
    )
```

```python
import functools

import jax
import jax.numpy as jnp
from jax import lax
from jax.experimental import pallas as pl
from jax.experimental.pallas import tpu as pltpu
from jax.sharding import PartitionSpec as P


TICKS = 6
PASSES = 4
SUB = 8
VMEM_BYTES = 16 * 1024 * 1024


def shifted(x, axis, by):
    count = lax.axis_size(axis)
    pairs = [(i, i + by) for i in range(count) if 0 <= i + by < count]
    return lax.ppermute(x, axis, pairs)


def passed_along(x, axis, by):
    count = lax.axis_size(axis)
    return lax.ppermute(x, axis, [(i, (i + by) % count) for i in range(count)])


def two_halves(x):
    high = x.astype(jnp.bfloat16)
    low = (x - high.astype(jnp.float32)).astype(jnp.bfloat16)
    return jnp.concatenate([high, low], axis=1)


def prep_kernel(x_ref, anchor_ref, left_ref, dx_ref, edge_ref, head_ref):
    series_x, _, _ = x_ref.shape
    pairs, levels, groups, _, tile = edge_ref.shape
    for m in range(series_x):
        x = x_ref[m].astype(jnp.float32)
        head_ref[m] = x[0:SUB]
        first = lax.broadcasted_iota(jnp.int32, x.shape, 0) == 0
        anchor = jnp.broadcast_to(anchor_ref[m : m + 1, :].astype(jnp.float32), x.shape)
        dx_ref[m] = (x - jnp.where(first, anchor, pltpu.roll(x, 1, 0))).astype(jnp.bfloat16)
    sub = lax.broadcasted_iota(jnp.int32, (SUB, tile), 0)
    lane = lax.broadcasted_iota(jnp.int32, (SUB, tile), 1)
    for p in range(pairs):
        for r in range(levels):
            row = jnp.broadcast_to(left_ref[p : p + 1, r * tile : (r + 1) * tile], (SUB, tile))
            for j in range(groups):
                own = jnp.where(lane == sub * groups + j, row, 0.0)
                edge_ref[p, r, j] = jnp.broadcast_to(
                    jnp.sum(own, axis=1, keepdims=True), (SUB, tile)
                )


def times_y(rows, y_all):
    return lax.dot_general(
        rows, y_all, (((1,), (1,)), ((), ())), preferred_element_type=jnp.float32
    )


def products_kernel(dx_ref, y_ref, *refs):
    out_ref = refs[-1]
    series_x = dx_ref.shape[0]
    series_y, tile, channels = y_ref.shape
    y_all = y_ref[...].reshape(series_y * tile, channels)
    for m in range(series_x):
        both = times_y(dx_ref[m], y_all)
        for n in range(series_y):
            out_ref[m * series_y + n] = both[:, n * tile : (n + 1) * tile]
        if len(refs) > 1:
            both = times_y(refs[0][m].astype(jnp.bfloat16), y_all)
            for n in range(series_y):
                out_ref[m * series_y + n, 0:1, :] = both[0:1, n * tile : (n + 1) * tile]


def tick_kernel(at, last, *refs):
    start_ref, products_ref, bottom_ref, before_ref, left_ref, *refs = refs
    if at == 0:
        dx_ref, y_ref, head_ref, received_ref, *refs = refs
    earlier_refs = []
    if last:
        earlier_refs, refs = refs[:at], refs[at:]
    out_ref, top_ref, *refs = refs
    if not last:
        after_ref, *refs = refs
    if at == 0:
        row_ref, *refs = refs
    (ones_ref,) = refs
    pairs, block_len, tile = products_ref.shape
    if at == 0:
        series_x, _, channels = dx_ref.shape
        series_y = y_ref.shape[0]
    levels = block_len // tile
    groups = tile // SUB
    at_start = start_ref[0] == 1

    if at == 0:
        for m in range(series_x):
            jump = head_ref[m] - received_ref[m].astype(jnp.float32)
            row_ref[m] = jnp.where(at_start, dx_ref[m, 0:SUB, :].astype(jnp.float32), jump)
    patch = [None] * pairs
    if at == 0:
        y_all = y_ref[...].reshape(series_y * tile, channels)
        for m in range(series_x):
            both = times_y(row_ref[m].astype(jnp.bfloat16), y_all)
            for n in range(series_y):
                seam = both[0:1, n * tile : (n + 1) * tile]
                patch[m * series_y + n] = jnp.broadcast_to(seam, (SUB, tile))

    row = lax.broadcasted_iota(jnp.int32, (2 * tile, tile), 0) % tile
    col = lax.broadcasted_iota(jnp.int32, (2 * tile, tile), 1)
    strict = (row < col).astype(jnp.float32).astype(jnp.bfloat16)
    inclusive = (row <= col).astype(jnp.float32).astype(jnp.bfloat16)
    ones_ref[:, :tile] = strict
    ones_ref[:, tile:] = inclusive
    sub = lax.broadcasted_iota(jnp.int32, (SUB, tile), 0)
    lane = lax.broadcasted_iota(jnp.int32, (SUB, tile), 1)

    def sum_before(total):
        out = jnp.where(sub >= 1, pltpu.roll(total, 1, 0), 0.0)
        step = 1
        while step < SUB - 1:
            out = out + jnp.where(sub >= step, pltpu.roll(out, step, 0), 0.0)
            step *= 2
        return out

    def over_sublanes(x):
        step = SUB // 2
        while step:
            x = x + pltpu.roll(x, step, 0)
            step //= 2
        return x

    def dot(a, b):
        return jnp.dot(a, b, preferred_element_type=jnp.float32)

    bottom, bottom_shift, corner = [], [], []
    for p in range(pairs):
        b = jnp.broadcast_to(bottom_ref[p : p + 1, :], (SUB, tile))
        b = jnp.where(at_start, 1.0, b)
        c = jnp.broadcast_to(before_ref[p : p + 1, tile - 1 : tile], (SUB, tile))
        c = jnp.where(at_start, 1.0, c)
        bottom.append(b)
        corner.append(c)
        if not last:
            after_ref[p : p + 1, :] = b[0:1]
        bottom_shift.append(jnp.where(lane == 0, c, pltpu.roll(b, 1, 1)))

    for r in range(levels):
        edge, end = [], []
        for p in range(pairs):
            left = [left_ref[p, r, j] for j in range(groups)]
            first = jnp.where(sub == 0, corner[p], pltpu.roll(left[-1], 1, 0))
            edge.append([x - corner[p] for x in [first] + left[:-1]])
            end.append(jnp.broadcast_to(left[-1][SUB - 1 : SUB, :], (SUB, tile)))
        node = [[e + bottom_shift[p] for e in edge[p]] for p in range(pairs)]
        for sweep in range(PASSES):
            weighted = [[] for _ in range(pairs)]
            for p in range(pairs):
                for j in range(groups):
                    incr = products_ref[p, pl.ds(r * tile + j, SUB, stride=groups), :]
                    if at == 0 and r == 0 and j == 0:
                        incr = jnp.where(sub == 0, patch[p], incr)
                    weighted[p].append(node[p][j] * incr)
            if sweep == PASSES - 1:
                break
            for p in range(pairs):
                along = dot(two_halves(jnp.concatenate(weighted[p], axis=0)), ones_ref[:, :tile])
                along = [along[j * SUB : (j + 1) * SUB] for j in range(groups)]
                running = [None, along[0]]
                for j in range(1, groups):
                    running.append(running[-1] + along[j])
                offset = sum_before(running[-1]) + bottom_shift[p]
                node[p] = [edge[p][0] + offset] + [
                    (running[j] + edge[p][j]) + offset for j in range(1, groups)
                ]
        for p in range(pairs):
            column = weighted[p]
            while len(column) > 1:
                column = [a + b for a, b in zip(column[::2], column[1::2])]
            column = over_sublanes(column[0])
            sums = dot(two_halves(column), ones_ref[...])
            lift = end[p] - corner[p]
            rows = [
                jnp.broadcast_to(jnp.sum(x, axis=1, keepdims=True), (SUB, tile))
                for x in weighted[p]
            ]
            running = [rows[0]]
            for j in range(1, groups):
                running.append(running[-1] + rows[j])
            far = jnp.broadcast_to(bottom[p][:, tile - 1 : tile], (SUB, tile)) - corner[p]
            offset = sum_before(running[-1]) + far
            right = [left_ref[p, r, j] + (running[j] + offset) for j in range(groups)]
            if last:
                found = None
                for j in range(groups):
                    here = jnp.where(lane == sub * groups + j, right[j], 0.0)
                    found = here if found is None else found + here
                found = over_sublanes(found)
                out_ref[p : p + 1, r * tile : (r + 1) * tile] = found[0:1]
            else:
                for j in range(groups):
                    out_ref[p, r, j] = right[j]
            bottom[p] = bottom[p] + lift + sums[:, tile:]
            bottom_shift[p] = bottom_shift[p] + lift + sums[:, :tile]
            corner[p] = end[p]
    for k, earlier_ref in enumerate(earlier_refs):
        top_ref[:, k * tile : (k + 1) * tile] = earlier_ref[...]
    begin = len(earlier_refs) * tile
    for p in range(pairs):
        top_ref[p : p + 1, begin : begin + tile] = bottom[p][0:1]


VMEM = pl.BlockSpec(memory_space=pltpu.VMEM)


def prepare(x_path, x_anchor, left_in, tile):
    pairs, block_len = left_in.shape
    edge = (pairs, block_len // tile, tile // SUB, SUB, tile)
    return pl.pallas_call(
        prep_kernel,
        out_shape=(
            jax.ShapeDtypeStruct(x_path.shape, jnp.bfloat16),
            jax.ShapeDtypeStruct(edge, jnp.float32),
            jax.ShapeDtypeStruct((x_path.shape[0], SUB, x_path.shape[2]), jnp.float32),
        ),
        in_specs=[VMEM] * 3,
        out_specs=(VMEM, VMEM, VMEM),
        compiler_params=pltpu.CompilerParams(vmem_limit_bytes=VMEM_BYTES),
        name="prep",
    )(x_path, x_anchor, left_in)


def all_products(dx, y, rows):
    series_x, block_len, _ = dx.shape
    series_y, tile, _ = y.shape
    pairs = series_x * series_y
    return pl.pallas_call(
        products_kernel,
        out_shape=jax.ShapeDtypeStruct((pairs, block_len, tile), jnp.float32),
        in_specs=[VMEM] * (2 + len(rows)),
        out_specs=VMEM,
        compiler_params=pltpu.CompilerParams(vmem_limit_bytes=VMEM_BYTES),
        name="products",
    )(dx, y, *rows)


def tick(at, last, start, products, bottom, before, left, first, tops):
    pairs, block_len, tile = products.shape
    edge = jax.ShapeDtypeStruct((pairs, tile), jnp.float32)
    if last:
        shapes = [
            jax.ShapeDtypeStruct((pairs, block_len), jnp.float32),
            jax.ShapeDtypeStruct((pairs, tile * (at + 1)), jnp.float32),
        ]
        first = first + tops
    else:
        shapes = [jax.ShapeDtypeStruct(left.shape, jnp.float32), edge, edge]
    if at == 0:
        shapes.append(jax.ShapeDtypeStruct(first[2].shape, jnp.float32))
    specs = [pl.BlockSpec(memory_space=pltpu.SMEM)] + [VMEM] * (4 + len(first))
    return pl.pallas_call(
        functools.partial(tick_kernel, at, last),
        out_shape=tuple(shapes),
        in_specs=specs,
        out_specs=(VMEM,) * len(shapes),
        scratch_shapes=[pltpu.VMEM((2 * tile, 2 * tile), jnp.bfloat16)],
        compiler_params=pltpu.CompilerParams(vmem_limit_bytes=VMEM_BYTES),
        name="tick",
    )(start, products, bottom, before, left, *first)


def local(x_path, x_anchor, y_steps, left_in, bottom_in, corner_in):
    tile = y_steps.shape[1]
    at_start = lax.axis_index("tm") == 0
    start = at_start.astype(jnp.int32).reshape(1)
    received = shifted(x_path[:, -1:, :], "tm", 1)
    y_next = passed_along(y_steps, "tm", 1)
    dx, left, head = prepare(x_path, x_anchor, left_in, tile)
    y_now, bottom = y_steps, bottom_in
    previous = jnp.broadcast_to(corner_in, bottom_in.shape)
    first, tops = [dx, y_steps, head, received], []
    products = all_products(dx, y_steps, [])
    for t in range(TICKS):
        last = t == TICKS - 1
        left, top, *rest = tick(t, last, start, products, bottom, previous, left, first, tops)
        if last:
            return left, top
        tops.append(top)
        previous = rest[0]
        if t == 0:
            rows, first = [rest[1]], []
        bottom = shifted(top, "tm", 1)
        y_now = y_next
        products = all_products(dx, y_now, rows)
        if t + 2 < TICKS:
            y_now, _ = lax.optimization_barrier((y_now, top))
            y_next = passed_along(y_now, "tm", 1)


def solution(mesh):
    placed = (
        P("pair", "tm", None),
        P("pair", None),
        P("pair", "tm", None),
        P("pair", "tm"),
        P("pair", "tm"),
        P("pair", "tm"),
    )
    return jax.shard_map(
        local,
        mesh=mesh,
        in_specs=placed,
        out_specs=(P("pair", "tm"), P("pair", "tm")),
        check_vma=False,
    )
```
